32 devices in a mesh: row: 16 (over z, x, core), feat: 2 (over y).
Axes of the slice: x: 2, y: 2, z: 4, core: 2. Of those that a mesh axis runs over, the one named last changes fastest.
Arguments:
- features: bfloat16 [65536, 8192], P('row', 'feat'), may hold values from -6 to 6
- coef: bfloat16 [8192], P('feat'), may hold values from -0.0625 to 0.0625
- labels: int32 [65536], P('row'), may hold values 0 or 1
- sign_bits: int32 [65536], P('row'), may hold values 0 or 1
- samples: int32 [16, 4096], P('row'), may hold values from 0 to 4095
Outputs:
- gradient: float32 [8192], P('feat')
- sketch: bfloat16 [4096, 8192], P('row', 'feat')
- gram: float32 [4096, 4096], P('row', 'feat')
The draws below stay inside these ranges and needn't reach their ends.
Inputs may be any that keep to these rules, and one draw needn't show every extreme that they name: `samples`: row index inside the block.
All inputs are finite; a program needn't handle non-finite values. No bound on the sum of `labels` or of `sign_bits` on one device may be relied on, other than what follows from the above.
Results may differ from the reference program's by a relative error of at most 0.017.
Values may be sent and summed in bfloat16 or wider, within the bound.
A program may use at most 192 MiB of HBM per device.

```python
import jax
import jax.numpy as jnp
from jax import lax

F = 8192
SKETCH = 4096
ROWS_DEV = 4096
BLOCKS = 16
TOTAL = 65536


def with_ends(values, stream_key, smallest, largest):
    dims = values.shape
    spot = [jax.random.randint(jax.random.fold_in(stream_key, axis), (), 0, dims[axis]) for axis in range(len(dims))]
    values = values.at[tuple(spot)].set(smallest)
    longest = dims.index(max(dims))
    spot[longest] = (spot[longest] + 1) % dims[longest]
    return values.at[tuple(spot)].set(largest)


def block_levels(key, extent, split, low, top_value):
    loudness = 1.0
    for position, shards_of in split:
        heights = jax.random.uniform(jax.random.fold_in(jax.random.fold_in(key, 6), position), (shards_of,), jnp.float32, low / len(split), top_value / len(split))
        loudness = loudness * jnp.repeat(jnp.exp(heights), extent[position] // shards_of).reshape((-1,) + (1,) * (len(extent) - 1 - position))
    return loudness


def gaussian(own_key, extent, spread, bound, shards=(), kind=jnp.bfloat16):
    drawn = jax.random.normal(own_key, extent, jnp.float32) * spread
    if len(shards) > 0:
        drawn = block_levels(own_key, extent, shards, -0.22, 0.18) * drawn
    return jnp.clip(drawn, min=-bound, max=bound).astype(kind)


def setup_inputs(seed: int = 0) -> dict:
    streams_of = jax.random.split(jax.random.key(seed), 6)
    return {
        "features": gaussian(streams_of[0], (TOTAL, F), 1.0, 6.0, ((0, 16), (1, 2))),
        "coef": gaussian(streams_of[1], (F,), F ** -0.5, 0.0625, ((0, 2),)),
        "labels": with_ends((jax.random.randint(streams_of[2], (TOTAL,), 0, 2) < 1).astype(jnp.int32), jax.random.fold_in(streams_of[2], 1), 0, 1),
        "sign_bits": with_ends((jax.random.randint(streams_of[3], (TOTAL,), 0, 2) < 1).astype(jnp.int32), jax.random.fold_in(streams_of[3], 1), 0, 1),
        "samples": with_ends(jax.random.randint(streams_of[4], (BLOCKS, SKETCH), 0, ROWS_DEV), jax.random.fold_in(streams_of[4], 1), 0, ROWS_DEV - 1).astype(jnp.int32),
    }


def sylvester(hadamard_order):
    positions = jnp.arange(hadamard_order, dtype=jnp.int32)
    bit_correlation = positions[:, None] & positions[None, :]
    parity_count = jnp.zeros_like(bit_correlation)
    for bit_pos in range(max(hadamard_order.bit_length() - 1, 0)):
        parity_count = parity_count + (bit_correlation >> bit_pos & 1)
    return (1 - 2 * (parity_count % 2)).astype(jnp.float32)

def transform_block(block_rows):
    big_order = 32
    small_order = block_rows.shape[0] // big_order
    high_table = sylvester(big_order)
    low_table = sylvester(small_order)
    shaped = block_rows.reshape(big_order, small_order, block_rows.shape[1])
    first_pass = jnp.einsum('ij,jkf->ikf', high_table, shaped, precision=lax.Precision.HIGHEST)
    second_pass = jnp.einsum('kl,ilf->ikf', low_table, first_pass, precision=lax.Precision.HIGHEST)
    return second_pass.reshape(block_rows.shape[0], block_rows.shape[1])

def reference(features, coef, labels, sign_bits, samples):
    margins = jnp.dot(features, coef, preferred_element_type=jnp.float32)
    probability = jax.nn.sigmoid(margins)
    row_scale = jnp.sqrt(probability * (1.0 - probability))
    residual = (probability - labels.astype(jnp.float32)).astype(jnp.bfloat16)
    root_total = jnp.sqrt(jnp.float32(TOTAL))
    gradient = jnp.dot(residual, features, preferred_element_type=jnp.float32) / root_total
    factors = (2.0 * sign_bits.astype(jnp.float32) - 1.0) * row_scale
    blocks = features.reshape(BLOCKS, ROWS_DEV, F)
    factor_blocks = factors.reshape(BLOCKS, ROWS_DEV)

    def add_block(carry, inputs):
        block_rows, block_factor, block_samples = inputs
        weighted = (block_factor[:, None] * block_rows.astype(jnp.float32)).astype(jnp.bfloat16)
        transformed = transform_block(weighted.astype(jnp.float32))
        picked = lax.optimization_barrier(jnp.take(transformed, block_samples, axis=0).astype(jnp.bfloat16))
        return (carry + picked.astype(jnp.float32), None)
    total_sum, unused = lax.scan(add_block, jnp.zeros((SKETCH, F), jnp.float32), (blocks, factor_blocks, samples))
    sketch = (total_sum / root_total).astype(jnp.bfloat16)
    gram = jnp.dot(sketch, sketch.T, preferred_element_type=jnp.float32) / F
    return (gradient, sketch, gram)
```

```python
import jax
import jax.numpy as jnp
from jax import lax
from jax.sharding import PartitionSpec as P


def ring_order(n):
    if n % 4:
        return list(range(n))
    out = [4 * z + c for z in range(n // 4) for c in (0, 1)]
    back = [4 * z + c for z in reversed(range(n // 4)) for c in (2, 3)]
    return out + back


def sampled_rows(rows, width):
    overlap = rows[:, None] & jnp.arange(width, dtype=jnp.int32)[None, :]
    parity = lax.population_count(overlap) & 1
    return (1 - 2 * parity).astype(jnp.bfloat16)


def sum_over(value, axis):
    n = lax.axis_size(axis)
    if n & (n - 1):
        return lax.psum(value, axis)
    step = 1
    while step < n:
        value = value + lax.ppermute(value, axis, [(i, i ^ step) for i in range(n)])
        step *= 2
    return value


def per_device(features, coef, labels, sign_bits, samples):
    n = lax.axis_size("row")
    groups = lax.axis_size("feat")
    rows_here, feat_here = features.shape
    all_features = feat_here * groups
    root_total = jnp.sqrt(jnp.float32(rows_here * n))
    order = ring_order(n)
    cw = [(order[i], order[(i + 1) % n]) for i in range(n)]
    ccw = [(order[(i + 1) % n], order[i]) for i in range(n)]
    place = [0] * n
    for i, device in enumerate(order):
        place[device] = i
    me = lax.axis_index("row")
    pos = jnp.asarray(place, jnp.int32)[me]
    order_table = jnp.asarray(order, jnp.int32)

    margins = sum_over(
        jnp.dot(features, coef, preferred_element_type=jnp.float32), "feat"
    )
    probability = jax.nn.sigmoid(margins)
    row_scale = jnp.sqrt(probability * (1.0 - probability))
    residual = (probability - labels.astype(jnp.float32)).astype(jnp.bfloat16)
    signs = 2.0 * sign_bits.astype(jnp.float32) - 1.0
    factor = (signs * row_scale)[:, None]
    half = feat_here // 2
    weighted = lax.optimization_barrier((factor * features).astype(jnp.bfloat16))

    depth = samples.shape[1] // n
    owners = order_table[(pos + jnp.arange(n, dtype=jnp.int32)) % n]
    near = jnp.take(samples[0].reshape(n, depth), owners, axis=0)

    def picked(rows):
        table = lax.optimization_barrier(sampled_rows(rows, rows_here))
        both = jnp.dot(table, weighted, preferred_element_type=jnp.float32)
        return lax.optimization_barrier(both.astype(jnp.bfloat16))

    def add(*terms):
        total = terms[0].astype(jnp.float32)
        for term in terms[1:]:
            total = total + term.astype(jnp.float32)
        return total

    h = n // 2
    pairs = [jnp.concatenate([near[h - s], near[(s - h + 1) % n]]) for s in range(h)]
    ahead_in, behind_in, own = None, None, None
    rows = pairs[0]
    for s in range(h):
        both = picked(rows)
        ahead, behind = both[:depth], both[depth:]
        if s:
            ahead = add(ahead, ahead_in).astype(jnp.bfloat16)
        if s < h - 1:
            if s:
                behind = add(behind, behind_in).astype(jnp.bfloat16)
            ahead, behind, rows = lax.optimization_barrier((ahead, behind, pairs[s + 1]))
            behind_in = lax.ppermute(behind, "row", ccw)
        else:
            own = behind
        ahead_in = lax.ppermute(ahead, "row", cw)
    parts = []
    for side in (0, 1):
        span = slice(side * half, (side + 1) * half)
        total = add(own[:, span], ahead_in[:, span], behind_in[:, span])
        parts.append((total / root_total).astype(jnp.bfloat16))
    sketch = jnp.concatenate(parts, axis=1)
    long_perm, short_perm = (cw, ccw), (ccw, cw)
    sign = (1, -1)

    grad_total = jnp.dot(residual, features, preferred_element_type=jnp.float32)
    gradient = sum_over(grad_total, "row") / root_total

    blocks = [{0: parts[0]}, {0: parts[1]}]
    grams, others = {}, {}
    swap = [(0, 1), (1, 0)]

    def gram_of(distance):
        a, b = blocks[0][distance], blocks[1][distance]
        dims = (((1,), (1,)), ((), ()))
        return lax.dot_general(
            parts[0], a, dims, preferred_element_type=jnp.float32
        ) + lax.dot_general(parts[1], b, dims, preferred_element_type=jnp.float32)

    def finish(distances):
        for d in distances:
            grams[d] = gram_of(d)
        if groups == 2:
            sent = jnp.concatenate(
                [grams[d].astype(jnp.bfloat16) for d in distances], axis=0
            )
            got = lax.ppermute(sent, "feat", swap)
            for i, d in enumerate(distances):
                others[d] = got[i * depth : (i + 1) * depth]

    for s in range(h):
        for side in (0, 1):
            prev, here = (-sign[side] * s) % n, (-sign[side] * (s + 1)) % n
            blocks[side][here] = lax.ppermute(
                blocks[side][prev], "row", long_perm[side]
            )
            if s < h - 1:
                prev, here = (sign[side] * s) % n, (sign[side] * (s + 1)) % n
                blocks[side][here] = lax.ppermute(
                    blocks[side][prev], "row", short_perm[side]
                )
        if s == 0:
            finish([0])
        if s < h - 1:
            finish([(s + 1) % n, (-s - 1) % n])
        else:
            finish([h])

    where = (jnp.asarray(place, jnp.int32) - pos) % n
    if groups == 2:
        stacked = jnp.stack([add(grams[d], others[d]) for d in range(n)])
        wanted = n // groups
        feat = lax.axis_index("feat")
        mine = lax.dynamic_slice_in_dim(where, feat * wanted, wanted)
        block = jnp.take(stacked, mine, axis=0) / all_features
        gram_block = block.transpose(1, 0, 2).reshape(depth, wanted * depth)
    else:
        stacked = jnp.stack([grams[d].astype(jnp.bfloat16) for d in range(n)])
        part = jnp.take(stacked, where, axis=0)
        part = part.transpose(1, 0, 2).reshape(depth, n * depth)
        gram_block = (
            lax.psum_scatter(part, "feat", scatter_dimension=1, tiled=True).astype(
                jnp.float32
            )
            / all_features
        )
    return (gradient, sketch, gram_block)


def solution(mesh):
    in_specs = (P("row", "feat"), P("feat"), P("row"), P("row"), P("row", None))
    out_specs = (P("feat"), P("row", "feat"), P("row", "feat"))
    return jax.shard_map(
        per_device, mesh=mesh, in_specs=in_specs, out_specs=out_specs, check_vma=False
    )
```

```python
import jax
import jax.numpy as jnp
from jax import lax
from jax.sharding import PartitionSpec as P


def ring_order(n):
    if n % 4:
        return list(range(n))
    out = [4 * z + c for z in range(n // 4) for c in (0, 1)]
    back = [4 * z + c for z in reversed(range(n // 4)) for c in (2, 3)]
    return out + back


def sampled_rows(rows, width):
    overlap = rows[:, None] & jnp.arange(width, dtype=jnp.int32)[None, :]
    parity = lax.population_count(overlap) & 1
    return (1 - 2 * parity).astype(jnp.bfloat16)


def sum_over(value, axis):
    n = lax.axis_size(axis)
    if n & (n - 1):
        return lax.psum(value, axis)
    step = 1
    while step < n:
        value = value + lax.ppermute(value, axis, [(i, i ^ step) for i in range(n)])
        step *= 2
    return value


def per_device(features, coef, labels, sign_bits, samples):
    n = lax.axis_size("row")
    groups = lax.axis_size("feat")
    rows_here, feat_here = features.shape
    all_features = feat_here * groups
    root_total = jnp.sqrt(jnp.float32(rows_here * n))
    order = ring_order(n)
    cw = [(order[i], order[(i + 1) % n]) for i in range(n)]
    ccw = [(order[(i + 1) % n], order[i]) for i in range(n)]
    place = [0] * n
    for i, device in enumerate(order):
        place[device] = i
    me = lax.axis_index("row")
    pos = jnp.asarray(place, jnp.int32)[me]
    order_table = jnp.asarray(order, jnp.int32)

    margins = sum_over(
        jnp.dot(features, coef, preferred_element_type=jnp.float32), "feat"
    )
    probability = jax.nn.sigmoid(margins)
    row_scale = jnp.sqrt(probability * (1.0 - probability))
    residual = (probability - labels.astype(jnp.float32)).astype(jnp.bfloat16)
    signs = 2.0 * sign_bits.astype(jnp.float32) - 1.0
    factor = (signs * row_scale)[:, None]
    half = feat_here // 2
    weighted = lax.optimization_barrier((factor * features).astype(jnp.bfloat16))

    depth = samples.shape[1] // n
    owners = order_table[(pos + jnp.arange(n, dtype=jnp.int32)) % n]
    near = jnp.take(samples[0].reshape(n, depth), owners, axis=0)

    def picked(rows):
        table = lax.optimization_barrier(sampled_rows(rows, rows_here))
        both = jnp.dot(table, weighted, preferred_element_type=jnp.float32)
        return lax.optimization_barrier(both.astype(jnp.bfloat16))

    def add(*terms):
        total = terms[0].astype(jnp.float32)
        for term in terms[1:]:
            total = total + term.astype(jnp.float32)
        return total

    h = n // 2
    pairs = [jnp.concatenate([near[h - s], near[(s - h + 1) % n]]) for s in range(h)]
    ahead_in, behind_in, own = None, None, None
    rows = pairs[0]
    for s in range(h):
        both = picked(rows)
        ahead, behind = both[:depth], both[depth:]
        if s:
            ahead = add(ahead, ahead_in).astype(jnp.bfloat16)
        if s < h - 1:
            if s:
                behind = add(behind, behind_in).astype(jnp.bfloat16)
            ahead, behind, rows = lax.optimization_barrier((ahead, behind, pairs[s + 1]))
            behind_in = lax.ppermute(behind, "row", ccw)
        else:
            own = behind
        ahead_in = lax.ppermute(ahead, "row", cw)
    parts = []
    for side in (0, 1):
        span = slice(side * half, (side + 1) * half)
        total = add(own[:, span], ahead_in[:, span], behind_in[:, span])
        parts.append((total / root_total).astype(jnp.bfloat16))
    grad_total = jnp.dot(residual, features, preferred_element_type=jnp.float32)
    parts[0], parts[1], grad_total = lax.optimization_barrier(
        (parts[0], parts[1], grad_total)
    )
    sketch = jnp.concatenate(parts, axis=1)
    long_perm, short_perm = (cw, ccw), (ccw, cw)
    sign = (1, -1)

    gradient = sum_over(grad_total, "row") / root_total

    blocks = [{0: parts[0]}, {0: parts[1]}]
    grams, others = {}, {}
    swap = [(0, 1), (1, 0)]

    def gram_of(distance):
        a, b = blocks[0][distance], blocks[1][distance]
        dims = (((1,), (1,)), ((), ()))
        return lax.dot_general(
            parts[0], a, dims, preferred_element_type=jnp.float32
        ) + lax.dot_general(parts[1], b, dims, preferred_element_type=jnp.float32)

    def finish(distances):
        for d in distances:
            grams[d] = gram_of(d)
        if groups == 2:
            sent = jnp.concatenate(
                [grams[d].astype(jnp.bfloat16) for d in distances], axis=0
            )
            got = lax.ppermute(sent, "feat", swap)
            for i, d in enumerate(distances):
                others[d] = got[i * depth : (i + 1) * depth]

    for s in range(h):
        for side in (0, 1):
            prev, here = (-sign[side] * s) % n, (-sign[side] * (s + 1)) % n
            blocks[side][here] = lax.ppermute(
                blocks[side][prev], "row", long_perm[side]
            )
            if s < h - 1:
                prev, here = (sign[side] * s) % n, (sign[side] * (s + 1)) % n
                blocks[side][here] = lax.ppermute(
                    blocks[side][prev], "row", short_perm[side]
                )
        if s == 0:
            finish([0])
        if s < h - 1:
            finish([(s + 1) % n, (-s - 1) % n])
        else:
            finish([h])

    where = (jnp.asarray(place, jnp.int32) - pos) % n
    if groups == 2:
        stacked = jnp.stack([add(grams[d], others[d]) for d in range(n)])
        wanted = n // groups
        feat = lax.axis_index("feat")
        mine = lax.dynamic_slice_in_dim(where, feat * wanted, wanted)
        block = jnp.take(stacked, mine, axis=0) / all_features
        gram_block = block.transpose(1, 0, 2).reshape(depth, wanted * depth)
    else:
        stacked = jnp.stack([grams[d].astype(jnp.bfloat16) for d in range(n)])
        part = jnp.take(stacked, where, axis=0)
        part = part.transpose(1, 0, 2).reshape(depth, n * depth)
        gram_block = (
            lax.psum_scatter(part, "feat", scatter_dimension=1, tiled=True).astype(
                jnp.float32
            )
            / all_features
        )
    return (gradient, sketch, gram_block)


def solution(mesh):
    in_specs = (P("row", "feat"), P("feat"), P("row"), P("row"), P("row", None))
    out_specs = (P("feat"), P("row", "feat"), P("row", "feat"))
    return jax.shard_map(
        per_device, mesh=mesh, in_specs=in_specs, out_specs=out_specs, check_vma=False
    )
```
